32 devices in a mesh: row: 4 (over y, x), col: 8 (over z, core).
Axes of the slice: x: 2, y: 2, z: 4, core: 2. Of those that a mesh axis runs over, the one named last changes fastest.
Arguments:
- ancestor_inverse: float32 [24576, 24576], P('row', 'col'), may hold values from -0.0546875 to 0.0546875
- lower_panel: float32 [2, 24576, 256], P(None, ('row', 'col')), may hold values from -6 to 6
- diag_factor: float32 [2, 256, 256], replicated, may hold values from -0.09375 to 0.09375
- diag_block: float32 [2, 256, 256], replicated, may hold values from -24 to 24
- pattern: int32 [2, 384], replicated, may hold values 0 or 1
Outputs:
- panel_inverse: float32 [2, 24576, 256], P(None, ('row', 'col'))
- diag_inverse: float32 [2, 256, 256], replicated
The draws below stay inside these ranges and needn't reach their ends.
All inputs are finite; a program needn't handle non-finite values.
Results may differ from the reference program's by a relative error of at most 0.000071.
Values sent between devices are 32-bit elements; how exact they have to be, the bound alone decides.
A program may use at most 192 MiB of HBM per device.

```python
import jax
import jax.numpy as jnp
from jax import lax

W = 256
A = 24576
BS = 64
NS = 2
ABLK = 384


def place_ends(result, stream_key, least, largest):
    shape = result.shape
    spot = [jax.random.randint(jax.random.fold_in(stream_key, axis), (), 0, shape[axis]) for axis in range(len(shape))]
    result = result.at[tuple(spot)].set(least)
    longest = shape.index(max(shape))
    spot[longest] = (spot[longest] + 1) % shape[longest]
    return result.at[tuple(spot)].set(largest)


def strengthened(drawn, stream_key, source, target, parts, factor):
    def block_of(position):
        return (jnp.arange(drawn.shape[position]) // (drawn.shape[position] // parts)).reshape((-1,) + (1,) * (drawn.ndim - 1 - position))

    one_side = jax.random.permutation(stream_key, parts)[block_of(target)]
    far = (block_of(target) + parts // 2) % parts
    return jnp.where((block_of(source) == one_side) | (block_of(source) == far), factor * drawn, drawn)


def levels(rng, extent, shards, smallest, largest):
    loudness, own = 1.0, jax.random.fold_in(rng, 6)
    for dim, blocks in shards:
        heights = jnp.exp(jax.random.uniform(jax.random.fold_in(own, dim), (blocks,), jnp.float32, smallest / len(shards), largest / len(shards)))
        loudness = loudness * jnp.repeat(heights, extent[dim] // blocks).reshape([-1 if axis == dim else 1 for axis in range(len(extent))])
    return loudness


def scatter_about(own_key, extent, scale, reach, cuts=(), held_as=jnp.bfloat16):
    loudness = levels(own_key, extent, cuts, -0.22, 0.18) if cuts else 1.0
    values = jax.random.normal(own_key, extent, jnp.float32) * scale * loudness
    return jnp.minimum(jnp.maximum(values, -reach), reach).astype(held_as)


def bell_draw_with(rng, extent, width, most, cuts, heavy, kind=jnp.bfloat16):
    values = width * jax.random.normal(rng, extent, jnp.float32)
    if cuts:
        values = values * levels(rng, extent, cuts, -0.22, 0.18)
    return jnp.clip(strengthened(values, jax.random.fold_in(rng, 3), *heavy), -most, most).astype(kind)


def setup_inputs(seed: int = 0) -> dict:
    splits = jax.random.split(jax.random.key(seed), 6)
    return {
        "ancestor_inverse": bell_draw_with(splits[0], (A, A), A ** -0.5, 0.0546875, ((0, 4), (1, 8)), (1, 0, 8, 2.0), jnp.float32),
        "lower_panel": scatter_about(splits[1], (NS, A, W), 1.0, 6.0, ((1, 32),), jnp.float32),
        "diag_factor": scatter_about(splits[2], (NS, W, W), (16 * W) ** -0.5, 0.09375, (), jnp.float32),
        "diag_block": scatter_about(splits[3], (NS, W, W), 4.0, 24.0, (), jnp.float32),
        "pattern": place_ends((jax.random.randint(splits[4], (NS, ABLK), 0, 2) < 1).astype(jnp.int32), jax.random.fold_in(splits[4], 1), 0, 1),
    }


def reference(ancestor_inverse, lower_panel, diag_factor, diag_block, pattern):
    highest = lax.Precision.HIGHEST
    row_mask = jnp.repeat(pattern, BS, axis=1).astype(jnp.float32)
    normed = jnp.einsum('saw,swv->sav', lower_panel, diag_factor, precision=highest) * row_mask[:, :, None]

    def single(normed_one):
        return jnp.dot(ancestor_inverse, normed_one, precision=highest, preferred_element_type=jnp.float32)

    product = lax.map(single, normed)
    panel_inverse = -product * row_mask[:, :, None]
    diag_inverse = diag_block - jnp.einsum('saw,sav->swv', normed, panel_inverse, precision=highest)
    return panel_inverse, diag_inverse
```

```python
import jax
import jax.numpy as jnp
from jax import lax
from jax.sharding import PartitionSpec as P

HIGHEST_PREC = lax.Precision.HIGHEST
HIGH_PREC = lax.Precision.HIGH


def local(ancestor_inverse, lower_panel, diag_factor, diag_block, pattern):
    row_count = lax.axis_size("row")
    col_count = lax.axis_size("col")
    row_index = lax.axis_index("row")
    col_index = lax.axis_index("col")
    snodes, piece_rows, width = lower_panel.shape
    tile_rows = row_count * col_count * piece_rows // pattern.shape[1]
    piece_start = (row_index * col_count + col_index) * piece_rows
    blocks = lax.dynamic_slice_in_dim(pattern, piece_start // tile_rows, piece_rows // tile_rows, 1)
    mask = jnp.repeat(blocks, tile_rows, axis=1).astype(jnp.float32)[:, :, None]
    normed = (
        jnp.einsum("spw,swv->spv", lower_panel, diag_factor, precision=HIGHEST_PREC) * mask
    )
    part_rows = piece_rows // row_count
    parts = normed.reshape(snodes, row_count, part_rows, width)
    number = (row_index * col_count + col_index) % row_count
    strips = []
    for snode in range(snodes):
        rounds = []
        for step in range(row_count):
            pairs = []
            for r in range(row_count):
                for c in range(col_count):
                    piece = r * col_count + c
                    q = (piece % row_count + step) % row_count
                    pairs.append((piece, q * col_count + piece // row_count))
            block = lax.dynamic_index_in_dim(parts[snode], (number + step) % row_count, 0, False)
            rounds.append(lax.ppermute(block, ("row", "col"), pairs))
        order = (row_index - jnp.arange(row_count)) % row_count
        received = jnp.take(jnp.stack(rounds), order, axis=0)
        everything = lax.all_gather(received, "row", axis=0)
        strips.append(jnp.swapaxes(everything, 0, 1).reshape(row_count * piece_rows, width))
    panels = []
    for snode in range(snodes):
        product = jnp.dot(ancestor_inverse, strips[snode], precision=HIGH_PREC)
        share = lax.psum_scatter(product, "col", scatter_dimension=0, tiled=True)
        panels.append(-share * mask[snode])
    panel_inverse = jnp.stack(panels)
    partial = jnp.einsum("spw,spv->swv", normed, panel_inverse, precision=HIGHEST_PREC)
    diag_inverse = diag_block - lax.psum(partial, ("row", "col"))
    return panel_inverse, diag_inverse


def solution(mesh):
    return jax.shard_map(
        local,
        mesh=mesh,
        in_specs=(P("row", "col"), P(None, ("row", "col"), None), P(), P(), P()),
        out_specs=(P(None, ("row", "col"), None), P()),
        check_vma=False,
    )
```

```python
import jax
import jax.numpy as jnp
from jax import lax
from jax.sharding import PartitionSpec as P

HIGHEST_PREC = lax.Precision.HIGHEST
HIGH_PREC = lax.Precision.HIGH


def sum_everywhere(value):
    count = lax.axis_size("row") * lax.axis_size("col")
    rows = value.shape[0] * value.shape[1]
    if count & (count - 1) or rows % count:
        return lax.psum(value, ("row", "col"))
    index = lax.axis_index("row") * lax.axis_size("col") + lax.axis_index("col")
    total = count.bit_length() - 1
    bits = [0] + list(range(total - 1, 0, -1))
    held = value.reshape(rows, value.shape[2])
    for bit in bits:
        pairs = [(d, d ^ (1 << bit)) for d in range(count)]
        half = held.shape[0] // 2
        upper = (index >> bit) & 1 == 1
        kept = jnp.where(upper, held[half:], held[:half])
        sent = jnp.where(upper, held[:half], held[half:])
        held = kept + lax.ppermute(sent, ("row", "col"), pairs)
    for bit in reversed(bits):
        pairs = [(d, d ^ (1 << bit)) for d in range(count)]
        other = lax.ppermute(held, ("row", "col"), pairs)
        upper = (index >> bit) & 1 == 1
        held = jnp.concatenate([jnp.where(upper, other, held), jnp.where(upper, held, other)], axis=0)
    return held.reshape(value.shape)


def local(ancestor_inverse, lower_panel, diag_factor, diag_block, pattern):
    row_count = lax.axis_size("row")
    col_count = lax.axis_size("col")
    row_index = lax.axis_index("row")
    col_index = lax.axis_index("col")
    snodes, piece_rows, width = lower_panel.shape
    tile_rows = row_count * col_count * piece_rows // pattern.shape[1]
    piece_start = (row_index * col_count + col_index) * piece_rows
    blocks = lax.dynamic_slice_in_dim(pattern, piece_start // tile_rows, piece_rows // tile_rows, 1)
    mask = jnp.repeat(blocks, tile_rows, axis=1).astype(jnp.float32)[:, :, None]
    normed = (
        jnp.einsum("spw,swv->spv", lower_panel, diag_factor, precision=HIGHEST_PREC) * mask
    )
    part_rows = piece_rows // row_count
    parts = normed.reshape(snodes, row_count, part_rows, width)
    number = (row_index * col_count + col_index) % row_count
    strips = []
    for snode in range(snodes):
        rounds = []
        for step in range(row_count):
            pairs = []
            for r in range(row_count):
                for c in range(col_count):
                    piece = r * col_count + c
                    q = (piece % row_count + step) % row_count
                    pairs.append((piece, q * col_count + piece // row_count))
            block = lax.dynamic_index_in_dim(parts[snode], (number + step) % row_count, 0, False)
            rounds.append(lax.ppermute(block, ("row", "col"), pairs))
        order = (row_index - jnp.arange(row_count)) % row_count
        received = jnp.take(jnp.stack(rounds), order, axis=0)
        everything = lax.all_gather(received, "row", axis=0)
        strips.append(jnp.swapaxes(everything, 0, 1).reshape(row_count * piece_rows, width))
    panels = []
    for snode in range(snodes):
        product = jnp.dot(ancestor_inverse, strips[snode], precision=HIGH_PREC)
        share = lax.psum_scatter(product, "col", scatter_dimension=0, tiled=True)
        panels.append(-share * mask[snode])
    panel_inverse = jnp.stack(panels)
    partial = jnp.einsum("spw,spv->swv", normed, panel_inverse, precision=HIGHEST_PREC)
    diag_inverse = diag_block - sum_everywhere(partial)
    return panel_inverse, diag_inverse


def solution(mesh):
    return jax.shard_map(
        local,
        mesh=mesh,
        in_specs=(P("row", "col"), P(None, ("row", "col"), None), P(), P(), P()),
        out_specs=(P(None, ("row", "col"), None), P()),
        check_vma=False,
    )
```
